32 devices in a mesh: groups: 2 (over y), member: 4 (over x, core), fsdp: 4 (over z).
Axes of the slice: x: 2, y: 2, z: 4, core: 2. Of those that a mesh axis runs over, the one named last changes fastest.
Arguments:
- params: float32 [64, 1024, 1024], P(('groups', 'member'), 'fsdp'), parts along dimension 0, may hold values from -210 to 210
- gradients: bfloat16 [64, 1024, 1024], P(('groups', 'member'), 'fsdp'), parts along dimension 0, may hold values from -1.5258789e-05 to 1.5258789e-05
- first_moment: float32 [64, 1024, 1024], P(('groups', 'member'), 'fsdp'), parts along dimension 0, may hold values from -5.9604645e-07 to 5.9604645e-07
- second_moment: float32 [64, 1024, 1024], P(('groups', 'member'), 'fsdp'), parts along dimension 0, may hold values from 1.8189895e-15 to 3.6379787e-14
Outputs:
- new_params: float32 [64, 1024, 1024], P(('groups', 'member'), 'fsdp'), parts along dimension 0
- new_first: float32 [64, 1024, 1024], P(('groups', 'member'), 'fsdp'), parts along dimension 0
- new_second: float32 [64, 1024, 1024], P(('groups', 'member'), 'fsdp'), parts along dimension 0
- update: float32 [64, 1024, 1024], P(('groups', 'member'), 'fsdp'), parts along dimension 0
- stein_dir: float32 [64, 1024, 1024], P(('groups', 'member'), 'fsdp'), parts along dimension 0
- pair_distance: float32 [64, 32], P('groups'), parts along dimension 0
The draws below stay inside these ranges and needn't reach their ends.
There are 2 independent parts, one for each index of `groups`. The reference program is written for one: setup_inputs(seed, part) draws one part's arguments, and reference() takes and returns one part's arrays. A program takes and returns all parts, laid end to end along the dimension named above; each array names one. Nothing has to cross between parts.
All inputs are finite; a program needn't handle non-finite values.
Results may differ from the reference program's by a relative error of at most 0.0025.
Values may be sent and summed in bfloat16 or wider, within the bound.
No kernel may reach another device: no remote copies, remote signals or barrier semaphores. Data moves between devices by JAX's collectives and lax.ppermute only.
A program may use at most 192 MiB of HBM per device.

```python
import math
import jax
import jax.numpy as jnp
from jax import lax

D = 1024
MEMBERS = 32
STEP_COUNT = 100
ROWS = 1024


def draw_params(key, part):
    key_coords = jax.random.fold_in(key, 101)
    key_directions = jax.random.fold_in(key, 102)
    key_jitter = jax.random.fold_in(key, 103)
    key_rows = jax.random.fold_in(key, 104)
    key_cols = jax.random.fold_in(key, 105)
    coords = jax.random.uniform(key_coords, (MEMBERS, 6), jnp.float32, -1.0, 1.0)
    directions = jax.random.truncated_normal(key_directions, -4.0, 4.0, (6, ROWS, D), jnp.float32)
    jitter = jax.random.truncated_normal(key_jitter, -4.0, 4.0, (MEMBERS, ROWS, D), jnp.float32)
    half_decade = 0.5 * math.log(10.0)
    row_rough = jnp.exp(jax.random.uniform(key_rows, (ROWS, 1), jnp.float32, 0.0, half_decade))
    col_rough = jnp.exp(jax.random.uniform(key_cols, (1, D), jnp.float32, 0.0, half_decade))
    position = jnp.arange(ROWS, dtype=jnp.float32)[:, None] / ROWS
    rising = jnp.sqrt(1.0 + 2.0 * position)
    spread_map = 0.25 * row_rough * col_rough * rising
    shaped = 0.7 * jitter
    for coord_idx in range(6):
        shaped = shaped + coords[:, coord_idx][:, None, None] * directions[coord_idx][None, :, :]
    result = spread_map[None, :, :] * shaped
    return result


def steps_of(own_key, dims, pieces, low, high):
    factor_of, own = 1.0, jax.random.fold_in(own_key, 6)
    for dim, shards_of in pieces:
        draws = jnp.exp(jax.random.uniform(jax.random.fold_in(own, dim), (shards_of,), jnp.float32, low / len(pieces), high / len(pieces)))
        factor_of = factor_of * jnp.repeat(draws, dims[dim] // shards_of).reshape([-1 if axis == dim else 1 for axis in range(len(dims))])
    return factor_of


def centred(rng, dims, scale, limit, split=(), kind=jnp.bfloat16):
    drawn = scale * jax.random.normal(rng, dims, jnp.float32)
    if split:
        drawn = drawn * steps_of(rng, dims, split, -0.22, 0.18)
    return jnp.clip(drawn, -limit, limit).astype(kind)


def setup_inputs(seed: int = 0, part: int = 0) -> dict:
    splits = jax.random.split(jax.random.key(seed), 5)
    part_keys = jax.random.split(jax.random.fold_in(splits[4], part), 5)
    params = draw_params(jax.random.fold_in(jax.random.fold_in(splits[4], part), 71), part)
    gradients = centred(part_keys[1], (MEMBERS, ROWS, D), (3.0 / (ROWS * D)), 1.52587890625e-05, ((0, 4), (1, 4)))
    first_moment = centred(part_keys[2], (MEMBERS, ROWS, D), (0.1 / (ROWS * D)), 5.960464477539062e-07, ((0, 4), (1, 4)), jnp.float32)
    second_moment = jnp.clip(jnp.exp(math.log(3.63797872577655e-14) - 2.9957322 * jax.random.uniform(part_keys[3], (MEMBERS, ROWS, D), jnp.float32) ** steps_of(part_keys[3], (MEMBERS, ROWS, D), ((0, 4), (1, 4)), -0.2, 0.2)), 1.818989489943217e-15, 3.63797872577655e-14)
    return {"params": params, "gradients": gradients, "first_moment": first_moment, "second_moment": second_moment}


decay_first = 0.9
decay_second = 0.95
epsilon = 1e-08
learn_rate = 0.001
weight_decay = 0.05

def kernel_from(gram_total, members):
    self_dots = jnp.diagonal(gram_total)
    sqdist = self_dots[:, None] + self_dots[None, :] - 2.0 * gram_total
    kernel_scale = jnp.sum(sqdist) / (members * (members - 1)) / math.log(members)
    kernel = jnp.exp(-sqdist / kernel_scale)
    return (sqdist, kernel_scale, kernel.astype(jnp.bfloat16))

def adamw_step(params, stein_dir, first_moment, second_moment):
    descent = -stein_dir
    new_first = decay_first * first_moment + (1.0 - decay_first) * descent
    new_second = decay_second * second_moment + (1.0 - decay_second) * descent * descent
    first_hat = new_first / (1.0 - decay_first ** STEP_COUNT)
    second_hat = new_second / (1.0 - decay_second ** STEP_COUNT)
    update = first_hat / (jnp.sqrt(second_hat) + epsilon) + weight_decay * params
    new_params = params - learn_rate * update
    return (new_params, new_first, new_second, update)

def reference(params, gradients, first_moment, second_moment):
    members = params.shape[0]
    working = params.astype(jnp.bfloat16)
    flat_work = working.reshape(members, -1)
    flat_ascent = (-gradients).reshape(members, -1)
    gram_total = jnp.dot(flat_work, flat_work.T, preferred_element_type=jnp.float32)
    sqdist, kernel_scale, kernel_half = kernel_from(gram_total, members)
    rowsum = lax.optimization_barrier(jnp.sum(kernel_half.astype(jnp.float32), axis=1))
    mixed_ascent = jnp.dot(kernel_half, flat_ascent, preferred_element_type=jnp.float32)
    mixed_work = jnp.dot(kernel_half, flat_work, preferred_element_type=jnp.float32)
    repulse = 2.0 / kernel_scale
    stein_mix = (mixed_ascent + repulse * (rowsum[:, None] * flat_work.astype(jnp.float32) - mixed_work)) / members
    stein_dir = stein_mix.reshape(params.shape)
    new_params, new_first, new_second, update = adamw_step(params, stein_dir, first_moment, second_moment)
    pair_distance = sqdist / (ROWS * D)
    return (new_params, new_first, new_second, update, stein_dir, pair_distance)
```

```python
import functools
import math

import jax
import jax.numpy as jnp
from jax import lax
from jax.experimental import pallas as pl
from jax.experimental.pallas import tpu as pltpu
from jax.sharding import PartitionSpec as P

STEP_COUNT = 100

decay_first = 0.9
decay_second = 0.95
epsilon = 1e-08
learn_rate = 0.001
weight_decay = 0.05

VMEM_BYTES = 48 << 20


def swap(x, axis, flip):
    return lax.ppermute(x, axis, [(i, i ^ flip) for i in range(lax.axis_size(axis))])


def tied(x, after):
    return lax.optimization_barrier((x, after))[0]


def sum_over(x, axis):
    stride, size = 1, lax.axis_size(axis)
    while stride < size:
        if size // stride >= 4:
            one, two, three = (swap(x, axis, flip * stride) for flip in (1, 2, 3))
            x = (x + one) + (two + three)
            stride *= 4
        else:
            x = x + swap(x, axis, stride)
            stride *= 2
    return x


def owner_matrix(me, n_member, members_dev, block_rows, dtype):
    members = n_member * members_dev
    stacked = lax.broadcasted_iota(jnp.int32, (members * block_rows, members), 0)
    column = lax.broadcasted_iota(jnp.int32, (members * block_rows, members), 1)
    slot = stacked // block_rows
    owner = ((slot // members_dev) ^ me) * members_dev + slot % members_dev
    return jnp.where(owner == column, 1.0, 0.0).astype(dtype)


def same_row(size, block_rows):
    left = lax.broadcasted_iota(jnp.int32, (size, size), 0) % block_rows
    right = lax.broadcasted_iota(jnp.int32, (size, size), 1) % block_rows
    return left == right


def stack_pieces(refs):
    parts = []
    for ref in refs:
        members_dev, block_rows, width = ref.shape
        parts.append(ref[...].astype(jnp.bfloat16).reshape(members_dev * block_rows, width))
    return jnp.concatenate(parts, axis=0)


def gram_kernel(me_ref, *refs):
    *piece_refs, gram_ref, acc_ref = refs
    step = pl.program_id(0)
    members_dev, block_rows, _ = piece_refs[0].shape
    n_member = len(piece_refs)

    @pl.when(step == 0)
    def _():
        acc_ref[...] = jnp.zeros_like(acc_ref)

    stacked = stack_pieces(piece_refs)
    acc_ref[...] += lax.dot_general(
        stacked, stacked, (((1,), (1,)), ((), ())), preferred_element_type=jnp.float32
    )

    @pl.when(step == pl.num_programs(0) - 1)
    def _():
        size = acc_ref.shape[0]
        owner = owner_matrix(me_ref[0], n_member, members_dev, block_rows, jnp.float32)
        kept = jnp.where(same_row(size, block_rows), acc_ref[...], 0.0)
        half = jnp.dot(kept, owner, precision=lax.Precision.HIGHEST)
        gram_ref[...] = lax.dot_general(
            owner, half, (((0,), (0,)), ((), ())), precision=lax.Precision.HIGHEST
        )


def local_gram(me, params, work_pieces):
    members_dev, rows_piece, width = work_pieces[0].shape
    n_member = len(work_pieces) + 1
    members = n_member * members_dev
    block_rows = min(16, rows_piece)
    steps = rows_piece // block_rows
    block = (members_dev, block_rows, width)
    size = members * block_rows
    return pl.pallas_call(
        gram_kernel,
        out_shape=jax.ShapeDtypeStruct((members, members), jnp.float32),
        grid_spec=pltpu.PrefetchScalarGridSpec(
            num_scalar_prefetch=1,
            grid=(steps,),
            in_specs=[pl.BlockSpec(block, lambda i, me_ref: (0, me_ref[0] * steps + i, 0))]
            + [pl.BlockSpec(block, lambda i, me_ref: (0, i, 0))] * (n_member - 1),
            out_specs=pl.BlockSpec((members, members), lambda i, me_ref: (0, 0)),
            scratch_shapes=[pltpu.VMEM((size, size), jnp.float32)],
        ),
        compiler_params=pltpu.CompilerParams(vmem_limit_bytes=VMEM_BYTES),
        cost_estimate=pl.CostEstimate(
            flops=2 * size * size * width * steps,
            bytes_accessed=(2 * n_member + 2) * members_dev * rows_piece * width,
            transcendentals=0,
        ),
        name="gram",
    )(me, params, *work_pieces)


def distances(gram):
    members = gram.shape[0]
    row = lax.broadcasted_iota(jnp.int32, gram.shape, 0)
    column = lax.broadcasted_iota(jnp.int32, gram.shape, 1)
    diagonal = jnp.where(row == column, gram, 0.0)
    down = jnp.sum(diagonal, axis=1, keepdims=True)
    across = jnp.sum(diagonal, axis=0, keepdims=True)
    return down + across - 2.0 * gram


def mix_kernel(n_member, me_ref, gram_ref, *refs):
    work_refs, grad_refs = refs[:n_member], refs[n_member : 2 * n_member]
    out_refs = refs[2 * n_member : 3 * n_member]
    big_ref, rowsum_ref, repulse_ref = refs[3 * n_member :]
    members_dev, block_rows, width = out_refs[0].shape
    members = n_member * members_dev
    size = members * block_rows

    @pl.when(pl.program_id(0) == 0)
    def _():
        sqdist = distances(gram_ref[...])
        total = jnp.sum(jnp.sum(sqdist, axis=1, keepdims=True), axis=0, keepdims=True)
        kernel_scale = total / (members * (members - 1)) / math.log(members)
        kernel_half = jnp.exp(-sqdist / kernel_scale).astype(jnp.bfloat16)
        owner = owner_matrix(me_ref[0], n_member, members_dev, block_rows, jnp.bfloat16)
        tall = jnp.dot(owner, kernel_half, preferred_element_type=jnp.float32)
        square = lax.dot_general(
            tall.astype(jnp.bfloat16), owner, (((1,), (1,)), ((), ())),
            preferred_element_type=jnp.float32,
        )
        big_ref[...] = jnp.where(same_row(size, block_rows), square, 0.0).astype(jnp.bfloat16)
        rowsum_ref[...] = jnp.sum(tall, axis=1, keepdims=True)
        repulse_ref[...] = 2.0 / kernel_scale

    big = big_ref[...]
    work = stack_pieces(work_refs)
    grads = stack_pieces(grad_refs)
    mixed_grads = jnp.dot(big, grads, preferred_element_type=jnp.float32)
    mixed_work = jnp.dot(big, work, preferred_element_type=jnp.float32)
    stein = (
        repulse_ref[...] * (rowsum_ref[...] * work.astype(jnp.float32) - mixed_work) - mixed_grads
    ) * (1.0 / members)
    stein = stein.astype(jnp.bfloat16)
    part = members_dev * block_rows
    for piece, out_ref in enumerate(out_refs):
        out_ref[...] = stein[piece * part : (piece + 1) * part].reshape(out_ref.shape)


def mix(me, gram, params, work_pieces, gradients, grad_pieces, first_row):
    members_dev, rows_piece, width = work_pieces[0].shape
    rows = grad_pieces[0].shape[1]
    n_member = len(work_pieces) + 1
    members = n_member * members_dev
    block_rows = min(16, rows)
    steps = rows // block_rows
    block = (members_dev, block_rows, width)
    size = members * block_rows
    skip = first_row // block_rows
    per_piece = rows_piece // block_rows
    whole = pl.BlockSpec(block, lambda i, me_ref: (0, me_ref[0] * per_piece + skip + i, 0))
    part = pl.BlockSpec(block, lambda i, me_ref: (0, i, 0))
    return pl.pallas_call(
        functools.partial(mix_kernel, n_member),
        out_shape=[jax.ShapeDtypeStruct((members_dev, rows, width), jnp.bfloat16)] * n_member,
        grid_spec=pltpu.PrefetchScalarGridSpec(
            num_scalar_prefetch=1,
            grid=(steps,),
            in_specs=[pl.BlockSpec((members, members), lambda i, me_ref: (0, 0)), whole]
            + [pl.BlockSpec(block, lambda i, me_ref: (0, skip + i, 0))] * (n_member - 1)
            + [whole]
            + [part] * (n_member - 1),
            out_specs=[part] * n_member,
            scratch_shapes=[
                pltpu.VMEM((size, size), jnp.bfloat16),
                pltpu.VMEM((size, 1), jnp.float32),
                pltpu.VMEM((1, 1), jnp.float32),
            ],
        ),
        compiler_params=pltpu.CompilerParams(vmem_limit_bytes=VMEM_BYTES),
        cost_estimate=pl.CostEstimate(
            flops=4 * size * size * width * steps,
            bytes_accessed=(6 * n_member + 2) * members_dev * rows * width,
            transcendentals=members * members,
        ),
        name="mix",
    )(me, gram, params, *work_pieces, gradients, *grad_pieces)


def adamw_kernel(row_ref, params_ref, first_ref, second_ref, stein_ref, *refs):
    del row_ref
    new_params_ref, new_first_ref, new_second_ref, update_ref, stein_dir_ref = refs[-5:]
    params = params_ref[...]
    stein_dir = stein_ref[...].astype(jnp.float32)
    new_first = decay_first * first_ref[...] - (1.0 - decay_first) * stein_dir
    new_second = decay_second * second_ref[...] + (1.0 - decay_second) * stein_dir * stein_dir
    first_hat = new_first * (1.0 / (1.0 - decay_first**STEP_COUNT))
    second_hat = new_second * (1.0 / (1.0 - decay_second**STEP_COUNT))
    update = first_hat / (jnp.sqrt(second_hat) + epsilon) + weight_decay * params
    new_params_ref[...] = params - learn_rate * update
    new_first_ref[...] = new_first
    new_second_ref[...] = new_second
    update_ref[...] = update
    stein_dir_ref[...] = stein_dir


def adamw(row_block, params, first_moment, second_moment, stein, earlier):
    members_dev, rows, width = stein.shape
    block_members = math.gcd(members_dev, 2)
    block = (block_members, rows, width)
    home = pl.BlockSpec(block, lambda i, row_ref: (i, row_ref[0], 0))
    shape = jax.ShapeDtypeStruct(params.shape, jnp.float32)
    entries = members_dev * rows * width
    return pl.pallas_call(
        adamw_kernel,
        out_shape=[shape] * 5,
        grid_spec=pltpu.PrefetchScalarGridSpec(
            num_scalar_prefetch=1,
            grid=(members_dev // block_members,),
            in_specs=[home] * 3
            + [pl.BlockSpec(block, lambda i, row_ref: (i, 0, 0))]
            + [pl.BlockSpec(memory_space=pl.ANY)] * len(earlier),
            out_specs=[home] * 5,
        ),
        input_output_aliases={5 + idx: idx for idx in range(len(earlier))},
        compiler_params=pltpu.CompilerParams(vmem_limit_bytes=VMEM_BYTES),
        cost_estimate=pl.CostEstimate(
            flops=20 * entries, bytes_accessed=34 * entries, transcendentals=entries
        ),
        name="adamw",
    )(row_block, params, first_moment, second_moment, stein, *earlier)


def shards(params, gradients, first_moment, second_moment):
    members_dev, rows_dev, feature_width = params.shape
    n_member = lax.axis_size("member")
    entries = rows_dev * lax.axis_size("fsdp") * feature_width
    rows_piece = rows_dev // n_member
    n_part = 2 if rows_piece % 32 == 0 else 1
    rows_part = rows_piece // n_part
    me = lax.axis_index("member")
    me_table = me[None]
    order = [2, 3, 1] if n_member == 4 else list(range(1, n_member))

    def rows_of(array, flip, part, rows):
        start = (me ^ flip) * rows_piece + part * rows_part
        return lax.dynamic_slice(array, (0, start, 0), (members_dev, rows, feature_width))

    work, source = {}, params
    for flip in order:
        packed = rows_of(source, flip, 0, rows_piece).astype(jnp.bfloat16)
        work[flip] = swap(packed, "member", flip)
        source = tied(params, packed)
    flips = range(1, n_member)

    def send_gradients(part, after):
        arrived, source = {}, tied(gradients, after)
        for flip in order:
            packed = rows_of(source, flip, part, rows_part)
            arrived[flip] = swap(packed, "member", flip)
            source = tied(gradients, packed)
        return [arrived[flip] for flip in flips]

    grads = [send_gradients(0, packed)]
    work = [work[flip] for flip in flips]
    gram = sum_over(local_gram(me_table, params, work), "fsdp")
    grads += [send_gradients(part, gram) for part in range(1, n_part)]
    gram = sum_over(gram, "member")

    stein, back = [], []
    for part in range(n_part):
        pieces = mix(
            me_table, gram, params, work, gradients, grads[part], part * rows_part
        )
        stein.append(pieces[0])
        back.append({flip: swap(pieces[flip], "member", flip) for flip in order})

    outs = ()

    def finish(flip, part, piece, outs):
        row_block = ((me ^ flip) * n_part + part)[None]
        return adamw(row_block, params, first_moment, second_moment, piece, outs)

    near = [flip for flip in flips if flip == 1]
    far = [flip for flip in order if flip != 1]
    for part in range(n_part):
        outs = finish(0, part, stein[part], outs)
        for flip in near:
            outs = finish(flip, part, back[part][flip], outs)
    for part in range(n_part):
        for flip in far:
            outs = finish(flip, part, back[part][flip], outs)
    new_params, new_first, new_second, update, stein_dir = outs
    self_dots = jnp.diagonal(gram)
    sqdist = self_dots[:, None] + self_dots[None, :] - 2.0 * gram
    pair_distance = sqdist / entries
    return (new_params, new_first, new_second, update, stein_dir, pair_distance)


def solution(mesh):
    return jax.shard_map(
        shards,
        mesh=mesh,
        in_specs=(
            P(("groups", "member"), "fsdp", None),
            P(("groups", "member"), "fsdp", None),
            P(("groups", "member"), "fsdp", None),
            P(("groups", "member"), "fsdp", None),
        ),
        out_specs=(
            P(("groups", "member"), "fsdp", None),
            P(("groups", "member"), "fsdp", None),
            P(("groups", "member"), "fsdp", None),
            P(("groups", "member"), "fsdp", None),
            P(("groups", "member"), "fsdp", None),
            P("groups", None),
        ),
        check_vma=False,
    )
```

```python
import functools
import math

import jax
import jax.numpy as jnp
from jax import lax
from jax.experimental import pallas as pl
from jax.experimental.pallas import tpu as pltpu
from jax.sharding import PartitionSpec as P

STEP_COUNT = 100

decay_first = 0.9
decay_second = 0.95
epsilon = 1e-08
learn_rate = 0.001
weight_decay = 0.05

VMEM_BYTES = 48 << 20
LIGHT = pl.CostEstimate(flops=1024, bytes_accessed=1024, transcendentals=0)
STEP = pl.CostEstimate(flops=1024, bytes_accessed=1 << 20, transcendentals=0)


def swap(x, axis, flip):
    return lax.ppermute(x, axis, [(i, i ^ flip) for i in range(lax.axis_size(axis))])


def tied(x, after):
    return lax.optimization_barrier((x, after))[0]


def sum_over(x, axis, stride=1):
    size = lax.axis_size(axis)
    while stride < size:
        if size // stride >= 4:
            one, two, three = (swap(x, axis, flip * stride) for flip in (1, 2, 3))
            x = (x + one) + (two + three)
            stride *= 4
        else:
            x = x + swap(x, axis, stride)
            stride *= 2
    return x


def owner_matrix(me, n_member, members_dev, block_rows, dtype):
    members = n_member * members_dev
    stacked = lax.broadcasted_iota(jnp.int32, (members * block_rows, members), 0)
    column = lax.broadcasted_iota(jnp.int32, (members * block_rows, members), 1)
    slot = stacked // block_rows
    owner = ((slot // members_dev) ^ me) * members_dev + slot % members_dev
    return jnp.where(owner == column, 1.0, 0.0).astype(dtype)


def same_row(size, block_rows):
    left = lax.broadcasted_iota(jnp.int32, (size, size), 0) % block_rows
    right = lax.broadcasted_iota(jnp.int32, (size, size), 1) % block_rows
    return left == right


def stack_pieces(refs):
    parts = []
    for ref in refs:
        members_dev, block_rows, width = ref.shape
        parts.append(ref[...].astype(jnp.bfloat16).reshape(members_dev * block_rows, width))
    return jnp.concatenate(parts, axis=0)


def pack_kernel(me_ref, *refs):
    del me_ref
    for in_ref, out_ref in zip(refs[: len(refs) // 2], refs[len(refs) // 2 :]):
        out_ref[...] = in_ref[...].astype(out_ref.dtype)


def pack_rows(me, params, flips, rows):
    members_dev, _, width = params.shape
    block_members = max(1, members_dev // 2)
    block = (block_members, rows, width)
    return pl.pallas_call(
        pack_kernel,
        out_shape=[jax.ShapeDtypeStruct((members_dev, rows, width), jnp.bfloat16)] * len(flips),
        grid_spec=pltpu.PrefetchScalarGridSpec(
            num_scalar_prefetch=1,
            grid=(members_dev // block_members,),
            in_specs=[
                pl.BlockSpec(block, lambda i, me_ref, flip=flip: (i, me_ref[0] ^ flip, 0))
                for flip in flips
            ],
            out_specs=[pl.BlockSpec(block, lambda i, me_ref: (i, 0, 0))] * len(flips),
        ),
        compiler_params=pltpu.CompilerParams(vmem_limit_bytes=VMEM_BYTES),
        cost_estimate=LIGHT,
        name="pack",
    )(me, *[params] * len(flips))


def gram_kernel(me_ref, *refs):
    *piece_refs, gram_ref, acc_ref = refs
    step = pl.program_id(0)
    members_dev, block_rows, _ = piece_refs[0].shape
    n_member = len(piece_refs)

    @pl.when(step == 0)
    def _():
        acc_ref[...] = jnp.zeros_like(acc_ref)

    stacked = stack_pieces(piece_refs)
    acc_ref[...] += lax.dot_general(
        stacked, stacked, (((1,), (1,)), ((), ())), preferred_element_type=jnp.float32
    )

    @pl.when(step == pl.num_programs(0) - 1)
    def _():
        size = acc_ref.shape[0]
        owner = owner_matrix(me_ref[0], n_member, members_dev, block_rows, jnp.float32)
        kept = jnp.where(same_row(size, block_rows), acc_ref[...], 0.0)
        half = jnp.dot(kept, owner, precision=lax.Precision.HIGHEST)
        gram_ref[...] = lax.dot_general(
            owner, half, (((0,), (0,)), ((), ())), precision=lax.Precision.HIGHEST
        )


def local_gram(me, params, work_pieces):
    members_dev, rows_piece, width = work_pieces[0].shape
    n_member = len(work_pieces) + 1
    members = n_member * members_dev
    block_rows = min(16, rows_piece)
    steps = rows_piece // block_rows
    block = (members_dev, block_rows, width)
    size = members * block_rows
    return pl.pallas_call(
        gram_kernel,
        out_shape=jax.ShapeDtypeStruct((members, members), jnp.float32),
        grid_spec=pltpu.PrefetchScalarGridSpec(
            num_scalar_prefetch=1,
            grid=(steps,),
            in_specs=[pl.BlockSpec(block, lambda i, me_ref: (0, me_ref[0] * steps + i, 0))]
            + [pl.BlockSpec(block, lambda i, me_ref: (0, i, 0))] * (n_member - 1),
            out_specs=pl.BlockSpec((members, members), lambda i, me_ref: (0, 0)),
            scratch_shapes=[pltpu.VMEM((size, size), jnp.float32)],
        ),
        compiler_params=pltpu.CompilerParams(vmem_limit_bytes=VMEM_BYTES),
        cost_estimate=LIGHT,
        name="gram",
    )(me, params, *work_pieces)


def distances(gram):
    members = gram.shape[0]
    row = lax.broadcasted_iota(jnp.int32, gram.shape, 0)
    column = lax.broadcasted_iota(jnp.int32, gram.shape, 1)
    diagonal = jnp.where(row == column, gram, 0.0)
    down = jnp.sum(diagonal, axis=1, keepdims=True)
    across = jnp.sum(diagonal, axis=0, keepdims=True)
    return down + across - 2.0 * gram


def mix_kernel(n_member, me_ref, gram_ref, *refs):
    work_refs, grad_refs = refs[:n_member], refs[n_member : 2 * n_member]
    out_refs = refs[2 * n_member : 3 * n_member]
    big_ref, rowsum_ref, repulse_ref = refs[3 * n_member :]
    members_dev, block_rows, width = out_refs[0].shape
    members = n_member * members_dev
    size = members * block_rows

    @pl.when(pl.program_id(0) == 0)
    def _():
        sqdist = distances(gram_ref[...])
        total = jnp.sum(jnp.sum(sqdist, axis=1, keepdims=True), axis=0, keepdims=True)
        kernel_scale = total / (members * (members - 1)) / math.log(members)
        kernel_half = jnp.exp(-sqdist / kernel_scale).astype(jnp.bfloat16)
        owner = owner_matrix(me_ref[0], n_member, members_dev, block_rows, jnp.bfloat16)
        tall = jnp.dot(owner, kernel_half, preferred_element_type=jnp.float32)
        square = lax.dot_general(
            tall.astype(jnp.bfloat16), owner, (((1,), (1,)), ((), ())),
            preferred_element_type=jnp.float32,
        )
        big_ref[...] = jnp.where(same_row(size, block_rows), square, 0.0).astype(jnp.bfloat16)
        rowsum_ref[...] = jnp.sum(tall, axis=1, keepdims=True)
        repulse_ref[...] = 2.0 / kernel_scale

    big = big_ref[...]
    work = stack_pieces(work_refs)
    grads = stack_pieces(grad_refs)
    mixed_grads = jnp.dot(big, grads, preferred_element_type=jnp.float32)
    mixed_work = jnp.dot(big, work, preferred_element_type=jnp.float32)
    stein = (
        repulse_ref[...] * (rowsum_ref[...] * work.astype(jnp.float32) - mixed_work) - mixed_grads
    ) * (1.0 / members)
    stein = stein.astype(jnp.bfloat16)
    part = members_dev * block_rows
    for piece, out_ref in enumerate(out_refs):
        out_ref[...] = stein[piece * part : (piece + 1) * part].reshape(out_ref.shape)


def mix(me, gram, params, work_pieces, gradients, grad_pieces, first_row):
    members_dev, rows_piece, width = work_pieces[0].shape
    rows = min(piece.shape[1] for piece in grad_pieces)
    n_member = len(work_pieces) + 1
    members = n_member * members_dev
    block_rows = min(16, rows)
    steps = rows // block_rows
    block = (members_dev, block_rows, width)
    size = members * block_rows
    skip = first_row // block_rows
    per_piece = rows_piece // block_rows
    whole = pl.BlockSpec(block, lambda i, me_ref: (0, me_ref[0] * per_piece + skip + i, 0))
    part = pl.BlockSpec(block, lambda i, me_ref: (0, i, 0))
    arrived = pl.BlockSpec(block, lambda i, me_ref: (0, skip + i, 0))
    return pl.pallas_call(
        functools.partial(mix_kernel, n_member),
        out_shape=[jax.ShapeDtypeStruct((members_dev, rows, width), jnp.bfloat16)] * n_member,
        grid_spec=pltpu.PrefetchScalarGridSpec(
            num_scalar_prefetch=1,
            grid=(steps,),
            in_specs=[pl.BlockSpec((members, members), lambda i, me_ref: (0, 0)), whole]
            + [arrived] * (n_member - 1)
            + [whole]
            + [part if piece.shape[1] == rows else arrived for piece in grad_pieces],
            out_specs=[part] * n_member,
            scratch_shapes=[
                pltpu.VMEM((size, size), jnp.bfloat16),
                pltpu.VMEM((size, 1), jnp.float32),
                pltpu.VMEM((1, 1), jnp.float32),
            ],
        ),
        compiler_params=pltpu.CompilerParams(vmem_limit_bytes=VMEM_BYTES),
        cost_estimate=LIGHT,
        name="mix",
    )(me, gram, params, *work_pieces, gradients, *grad_pieces)


def adamw_kernel(row_ref, params_ref, first_ref, second_ref, stein_ref, *refs):
    del row_ref
    new_params_ref, new_first_ref, new_second_ref, update_ref, stein_dir_ref = refs[-5:]
    params = params_ref[...]
    stein_dir = stein_ref[...].astype(jnp.float32)
    new_first = decay_first * first_ref[...] - (1.0 - decay_first) * stein_dir
    new_second = decay_second * second_ref[...] + (1.0 - decay_second) * stein_dir * stein_dir
    first_hat = new_first * (1.0 / (1.0 - decay_first**STEP_COUNT))
    second_hat = new_second * (1.0 / (1.0 - decay_second**STEP_COUNT))
    update = first_hat / (jnp.sqrt(second_hat) + epsilon) + weight_decay * params
    new_params_ref[...] = params - learn_rate * update
    new_first_ref[...] = new_first
    new_second_ref[...] = new_second
    update_ref[...] = update
    stein_dir_ref[...] = stein_dir


def adamw(row_block, params, first_moment, second_moment, stein, earlier):
    members_dev, rows, width = stein.shape
    block_members = math.gcd(members_dev, 4)
    block = (block_members, rows, width)
    home = pl.BlockSpec(block, lambda i, row_ref: (i, row_ref[0], 0))
    shape = jax.ShapeDtypeStruct(params.shape, jnp.float32)
    return pl.pallas_call(
        adamw_kernel,
        out_shape=[shape] * 5,
        grid_spec=pltpu.PrefetchScalarGridSpec(
            num_scalar_prefetch=1,
            grid=(members_dev // block_members,),
            in_specs=[home] * 3
            + [pl.BlockSpec(block, lambda i, row_ref: (i, 0, 0))]
            + [pl.BlockSpec(memory_space=pl.ANY)] * len(earlier),
            out_specs=[home] * 5,
        ),
        input_output_aliases={5 + idx: idx for idx in range(len(earlier))},
        compiler_params=pltpu.CompilerParams(vmem_limit_bytes=VMEM_BYTES),
        cost_estimate=STEP,
        name="adamw",
    )(row_block, params, first_moment, second_moment, stein, *earlier)


def shards(params, gradients, first_moment, second_moment):
    members_dev, rows_dev, feature_width = params.shape
    n_member = lax.axis_size("member")
    entries = rows_dev * lax.axis_size("fsdp") * feature_width
    rows_piece = rows_dev // n_member
    n_part = 2 if rows_piece % 32 == 0 else 1
    rows_part = rows_piece // n_part
    me = lax.axis_index("member")
    me_table = me[None]
    flips = range(1, n_member)
    near = [flip for flip in flips if flip == 1]
    far = [2, 3] if n_member == 4 else list(flips)[1:]

    def rows_of(array, flip, part, rows):
        start = (me ^ flip) * rows_piece + part * rows_part
        return lax.dynamic_slice(array, (0, start, 0), (members_dev, rows, feature_width))

    grads = [{} for _ in range(n_part)]
    work = {}
    last = None

    def finish(flip, part, piece, outs):
        row_block = ((me ^ flip) * n_part + part)[None]
        return adamw(row_block, params, first_moment, second_moment, piece, outs)

    def send(array, flip, part, rows, after):
        source = array if after is None else tied(array, after)
        packed = rows_of(source, flip, part, rows).astype(jnp.bfloat16)
        return swap(packed, "member", flip), packed

    packed = pack_rows(me_table, params, far, rows_piece)
    for flip, piece in zip(far, packed):
        work[flip] = swap(piece, "member", flip)
    last = packed
    for flip in far[:1]:
        whole, last = send(gradients, flip, 0, rows_piece, last)
        for part in range(n_part):
            grads[part][flip] = whole
    for flip in near:
        last = (last, work[far[0]]) if far else last
        work[flip], last = send(params, flip, 0, rows_piece, last)
        whole, last = send(gradients, flip, 0, rows_piece, last)
        for part in range(n_part):
            grads[part][flip] = whole
    gram = local_gram(me_table, params, [work[flip] for flip in flips])
    gram = sum_over(tied(gram, last), "fsdp")
    for flip in near:
        gram = gram + swap(gram, "member", flip)
    last = gram
    for part in range(n_part):
        for flip in far[1:]:
            grads[part][flip], last = send(gradients, flip, part, rows_part, last)
    gram = sum_over(gram, "member", 2)
    work = [work[flip] for flip in flips]
    grads = [[piece[flip] for flip in flips] for piece in grads]

    stein = [
        mix(me_table, gram, params, work, gradients, grads[part], part * rows_part)
        for part in range(n_part)
    ]
    back = [
        {flip: swap(pieces[flip], "member", flip) for flip in far + near} for pieces in stein
    ]
    outs = ()
    for part in range(n_part):
        outs = finish(0, part, stein[part][0], outs)
        if part + 1 < n_part:
            for flip in near:
                outs = finish(flip, part, back[part][flip], outs)
    for part in range(n_part):
        if part + 1 == n_part:
            for flip in near:
                outs = finish(flip, part, back[part][flip], outs)
        for flip in far:
            outs = finish(flip, part, back[part][flip], outs)
    new_params, new_first, new_second, update, stein_dir = outs
    self_dots = jnp.diagonal(gram)
    sqdist = self_dots[:, None] + self_dots[None, :] - 2.0 * gram
    pair_distance = sqdist / entries
    return (new_params, new_first, new_second, update, stein_dir, pair_distance)


def solution(mesh):
    return jax.shard_map(
        shards,
        mesh=mesh,
        in_specs=(
            P(("groups", "member"), "fsdp", None),
            P(("groups", "member"), "fsdp", None),
            P(("groups", "member"), "fsdp", None),
            P(("groups", "member"), "fsdp", None),
        ),
        out_specs=(
            P(("groups", "member"), "fsdp", None),
            P(("groups", "member"), "fsdp", None),
            P(("groups", "member"), "fsdp", None),
            P(("groups", "member"), "fsdp", None),
            P(("groups", "member"), "fsdp", None),
            P("groups", None),
        ),
        check_vma=False,
    )
```

```python
import functools
import math

import jax
import jax.numpy as jnp
from jax import lax
from jax.experimental import pallas as pl
from jax.experimental.pallas import tpu as pltpu
from jax.sharding import PartitionSpec as P

STEP_COUNT = 100

decay_first = 0.9
decay_second = 0.95
epsilon = 1e-08
learn_rate = 0.001
weight_decay = 0.05

VMEM_BYTES = 48 << 20
LIGHT = pl.CostEstimate(flops=1024, bytes_accessed=1024, transcendentals=0)
STEP = pl.CostEstimate(flops=1024, bytes_accessed=1 << 20, transcendentals=0)


LAST_CUTS = [(0, 16), (16, 16)]


def swap(x, axis, flip):
    return lax.ppermute(x, axis, [(i, i ^ flip) for i in range(lax.axis_size(axis))])


def tied(x, after):
    return lax.optimization_barrier((x, after))[0]


def sum_over(x, axis, stride=1):
    size = lax.axis_size(axis)
    while stride < size:
        if size // stride >= 4:
            one, two, three = (swap(x, axis, flip * stride) for flip in (1, 2, 3))
            x = (x + one) + (two + three)
            stride *= 4
        else:
            x = x + swap(x, axis, stride)
            stride *= 2
    return x


def owner_matrix(me, n_member, members_dev, block_rows, dtype):
    members = n_member * members_dev
    stacked = lax.broadcasted_iota(jnp.int32, (members * block_rows, members), 0)
    column = lax.broadcasted_iota(jnp.int32, (members * block_rows, members), 1)
    slot = stacked // block_rows
    owner = ((slot // members_dev) ^ me) * members_dev + slot % members_dev
    return jnp.where(owner == column, 1.0, 0.0).astype(dtype)


def same_row(size, block_rows):
    left = lax.broadcasted_iota(jnp.int32, (size, size), 0) % block_rows
    right = lax.broadcasted_iota(jnp.int32, (size, size), 1) % block_rows
    return left == right


def stack_pieces(blocks):
    parts = []
    for block in blocks:
        members_dev, block_rows, width = block.shape
        parts.append(block.astype(jnp.bfloat16).reshape(members_dev * block_rows, width))
    return jnp.concatenate(parts, axis=0)


def pieces_of(refs, head_refs, step):
    blocks = [ref[...] for ref in refs]
    for head_ref in head_refs:
        blocks[-1] = jnp.where(step == 0, head_ref[...], blocks[-1])
    return stack_pieces(blocks)


def pack_kernel(me_ref, *refs):
    del me_ref
    for in_ref, out_ref in zip(refs[: len(refs) // 2], refs[len(refs) // 2 :]):
        skip = in_ref.shape[1] - out_ref.shape[1]
        out_ref[...] = in_ref[:, skip:, :].astype(out_ref.dtype)


def pack_rows(me, params, flips, skips):
    members_dev, rows_dev, width = params.shape
    rows = rows_dev // lax.axis_size("member")
    block_members = max(1, members_dev // 2)
    return pl.pallas_call(
        pack_kernel,
        out_shape=[
            jax.ShapeDtypeStruct((members_dev, rows - skip, width), jnp.bfloat16)
            for skip in skips
        ],
        grid_spec=pltpu.PrefetchScalarGridSpec(
            num_scalar_prefetch=1,
            grid=(members_dev // block_members,),
            in_specs=[
                pl.BlockSpec(
                    (block_members, rows, width),
                    lambda i, me_ref, flip=flip: (i, me_ref[0] ^ flip, 0),
                )
                for flip in flips
            ],
            out_specs=[
                pl.BlockSpec((block_members, rows - skip, width), lambda i, me_ref: (i, 0, 0))
                for skip in skips
            ],
        ),
        compiler_params=pltpu.CompilerParams(vmem_limit_bytes=VMEM_BYTES),
        cost_estimate=LIGHT,
        name="pack",
    )(me, *[params] * len(flips))


def gram_kernel(n_member, me_ref, *refs):
    *piece_refs, gram_ref, acc_ref = refs
    step = pl.program_id(0)
    members_dev, block_rows, _ = piece_refs[0].shape

    @pl.when(step == 0)
    def _():
        acc_ref[...] = jnp.zeros_like(acc_ref)

    stacked = pieces_of(piece_refs[:n_member], piece_refs[n_member:], step)
    acc_ref[...] += lax.dot_general(
        stacked, stacked, (((1,), (1,)), ((), ())), preferred_element_type=jnp.float32
    )

    @pl.when(step == pl.num_programs(0) - 1)
    def _():
        size = acc_ref.shape[0]
        owner = owner_matrix(me_ref[0], n_member, members_dev, block_rows, jnp.float32)
        kept = jnp.where(same_row(size, block_rows), acc_ref[...], 0.0)
        half = jnp.dot(kept, owner, precision=lax.Precision.HIGHEST)
        gram_ref[...] = lax.dot_general(
            owner, half, (((0,), (0,)), ((), ())), precision=lax.Precision.HIGHEST
        )


def local_gram(me, params, work_pieces, head):
    members_dev, rows_piece, width = work_pieces[0].shape
    n_member = len(work_pieces) + 1
    members = n_member * members_dev
    block_rows = min(16, rows_piece)
    steps = rows_piece // block_rows
    block = (members_dev, block_rows, width)
    size = members * block_rows
    return pl.pallas_call(
        functools.partial(gram_kernel, n_member),
        out_shape=jax.ShapeDtypeStruct((members, members), jnp.float32),
        grid_spec=pltpu.PrefetchScalarGridSpec(
            num_scalar_prefetch=1,
            grid=(steps,),
            in_specs=[pl.BlockSpec(block, lambda i, me_ref: (0, me_ref[0] * steps + i, 0))]
            + [pl.BlockSpec(block, lambda i, me_ref: (0, i, 0))] * (n_member - 2)
            + [pl.BlockSpec(block, lambda i, me_ref: (0, jnp.maximum(i - len(head), 0), 0))]
            + [pl.BlockSpec(block, lambda i, me_ref: (0, 0, 0))] * len(head),
            out_specs=pl.BlockSpec((members, members), lambda i, me_ref: (0, 0)),
            scratch_shapes=[pltpu.VMEM((size, size), jnp.float32)],
        ),
        compiler_params=pltpu.CompilerParams(vmem_limit_bytes=VMEM_BYTES),
        cost_estimate=LIGHT,
        name="gram",
    )(me, params, *work_pieces, *head)


def distances(gram):
    members = gram.shape[0]
    row = lax.broadcasted_iota(jnp.int32, gram.shape, 0)
    column = lax.broadcasted_iota(jnp.int32, gram.shape, 1)
    diagonal = jnp.where(row == column, gram, 0.0)
    down = jnp.sum(diagonal, axis=1, keepdims=True)
    across = jnp.sum(diagonal, axis=0, keepdims=True)
    return down + across - 2.0 * gram


def mix_kernel(n_member, n_head, cuts, entries, me_ref, gram_ref, *refs):
    work_refs, refs = refs[:n_member], refs[n_member:]
    head_refs, grad_refs = refs[:n_head], refs[n_head : n_head + n_member]
    n_out = n_member - 1 + len(cuts)
    distance_ref, big_ref, rowsum_ref, repulse_ref = refs[-4:]
    out_refs = refs[-4 - n_out : -4]
    members_dev, block_rows, width = out_refs[0].shape
    members = n_member * members_dev
    size = members * block_rows

    @pl.when(pl.program_id(0) == 0)
    def _():
        sqdist = distances(gram_ref[...])
        distance_ref[...] = sqdist / entries
        total = jnp.sum(jnp.sum(sqdist, axis=1, keepdims=True), axis=0, keepdims=True)
        kernel_scale = total / (members * (members - 1)) / math.log(members)
        kernel_half = jnp.exp(-sqdist / kernel_scale).astype(jnp.bfloat16)
        owner = owner_matrix(me_ref[0], n_member, members_dev, block_rows, jnp.bfloat16)
        tall = jnp.dot(owner, kernel_half, preferred_element_type=jnp.float32)
        square = lax.dot_general(
            tall.astype(jnp.bfloat16), owner, (((1,), (1,)), ((), ())),
            preferred_element_type=jnp.float32,
        )
        big_ref[...] = jnp.where(same_row(size, block_rows), square, 0.0).astype(jnp.bfloat16)
        rowsum_ref[...] = jnp.sum(tall, axis=1, keepdims=True)
        repulse_ref[...] = 2.0 / kernel_scale

    big = big_ref[...]
    work = pieces_of(work_refs, head_refs, pl.program_id(0))
    grads = stack_pieces([ref[...] for ref in grad_refs])
    mixed_grads = jnp.dot(big, grads, preferred_element_type=jnp.float32)
    mixed_work = jnp.dot(big, work, preferred_element_type=jnp.float32)
    stein = (
        repulse_ref[...] * (rowsum_ref[...] * work.astype(jnp.float32) - mixed_work) - mixed_grads
    ) * (1.0 / members)
    stein = stein.reshape(n_member, members_dev, block_rows, width)
    for piece, out_ref in enumerate(out_refs[: n_member - 1]):
        out_ref[...] = stein[piece].astype(jnp.bfloat16)
    for (first, rows), out_ref in zip(cuts, out_refs[n_member - 1 :]):
        if rows >= block_rows and len(cuts) == 1:
            out_ref[...] = stein[-1].astype(jnp.bfloat16)
            continue
        inner = first % block_rows

        @pl.when(pl.program_id(0) == first // block_rows)
        def _():
            out_ref[...] = stein[-1, :, inner : inner + rows].astype(jnp.bfloat16)


def mix(
    me, gram, params, work_pieces, head, gradients, grad_pieces, first_row, rows, cuts, earlier,
    entries,
):
    members_dev, rows_piece, width = work_pieces[0].shape
    n_member = len(work_pieces) + 1
    members = n_member * members_dev
    block_rows = min(16, rows)
    steps = rows // block_rows
    block = (members_dev, block_rows, width)
    size = members * block_rows
    skip = first_row // block_rows
    per_piece = rows_piece // block_rows
    own = pl.BlockSpec(block, lambda i, me_ref: (0, me_ref[0] * per_piece + skip + i, 0))
    whole = pl.BlockSpec(block, lambda i, me_ref: (0, skip + i, 0))
    part = pl.BlockSpec(block, lambda i, me_ref: (0, i, 0))

    def fixed(count):
        return pl.BlockSpec((members_dev, count, width), lambda i, me_ref: (0, 0, 0))

    n_head = len(head)
    late = pl.BlockSpec(block, lambda i, me_ref: (0, jnp.maximum(skip + i - n_head, 0), 0))
    if first_row:
        head = []
    out_rows = [rows if piece else rows_piece for piece in range(n_member - 1)]
    out_rows += [count for _, count in cuts]
    return pl.pallas_call(
        functools.partial(mix_kernel, n_member, len(head), cuts, entries),
        out_shape=[
            jax.ShapeDtypeStruct((members_dev, count, width), jnp.bfloat16) for count in out_rows
        ]
        + [jax.ShapeDtypeStruct((members, members), jnp.float32)],
        grid_spec=pltpu.PrefetchScalarGridSpec(
            num_scalar_prefetch=1,
            grid=(steps,),
            in_specs=[pl.BlockSpec((members, members), lambda i, me_ref: (0, 0)), own]
            + [whole] * (n_member - 2)
            + [late]
            + [fixed(block_rows)] * len(head)
            + [own]
            + [part if piece.shape[1] == rows else whole for piece in grad_pieces]
            + [pl.BlockSpec(memory_space=pl.ANY)] * len(earlier),
            out_specs=[part if piece else whole for piece in range(n_member - 1)]
            + [part if len(cuts) == 1 else fixed(count) for _, count in cuts]
            + [pl.BlockSpec((members, members), lambda i, me_ref: (0, 0))],
            scratch_shapes=[
                pltpu.VMEM((size, size), jnp.bfloat16),
                pltpu.VMEM((size, 1), jnp.float32),
                pltpu.VMEM((1, 1), jnp.float32),
            ],
        ),
        input_output_aliases={
            2 + 2 * n_member + len(head) + idx: idx for idx in range(len(earlier))
        },
        compiler_params=pltpu.CompilerParams(vmem_limit_bytes=VMEM_BYTES),
        cost_estimate=LIGHT,
        name="mix",
    )(me, gram, params, *work_pieces, *head, gradients, *grad_pieces, *earlier)


def adamw_kernel(row_ref, params_ref, first_ref, second_ref, stein_ref, *refs):
    del row_ref
    new_params_ref, new_first_ref, new_second_ref, update_ref, stein_dir_ref = refs[-5:]
    params = params_ref[...]
    stein_dir = stein_ref[...].astype(jnp.float32)
    new_first = decay_first * first_ref[...] - (1.0 - decay_first) * stein_dir
    new_second = decay_second * second_ref[...] + (1.0 - decay_second) * stein_dir * stein_dir
    first_hat = new_first * (1.0 / (1.0 - decay_first**STEP_COUNT))
    second_hat = new_second * (1.0 / (1.0 - decay_second**STEP_COUNT))
    update = first_hat / (jnp.sqrt(second_hat) + epsilon) + weight_decay * params
    new_params_ref[...] = params - learn_rate * update
    new_first_ref[...] = new_first
    new_second_ref[...] = new_second
    update_ref[...] = update
    stein_dir_ref[...] = stein_dir


def adamw(row_block, params, first_moment, second_moment, stein, earlier):
    members_dev, rows, width = stein.shape
    block_members = math.gcd(members_dev, 4 if rows > 16 else 8)
    block_rows = rows if rows != 16 else 8
    block = (block_members, block_rows, width)
    steps = rows // block_rows
    home = pl.BlockSpec(block, lambda i, j, row_ref: (i, row_ref[0] * steps + j, 0))
    shape = jax.ShapeDtypeStruct(params.shape, jnp.float32)
    return pl.pallas_call(
        adamw_kernel,
        out_shape=[shape] * 5,
        grid_spec=pltpu.PrefetchScalarGridSpec(
            num_scalar_prefetch=1,
            grid=(members_dev // block_members, steps),
            in_specs=[home] * 3
            + [pl.BlockSpec(block, lambda i, j, row_ref: (i, j, 0))]
            + [pl.BlockSpec(memory_space=pl.ANY)] * len(earlier),
            out_specs=[home] * 5,
        ),
        input_output_aliases={5 + idx: idx for idx in range(len(earlier))},
        compiler_params=pltpu.CompilerParams(vmem_limit_bytes=VMEM_BYTES),
        cost_estimate=STEP,
        name="adamw",
    )(row_block, params, first_moment, second_moment, stein, *earlier)


def shards(params, gradients, first_moment, second_moment):
    members_dev, rows_dev, feature_width = params.shape
    n_member = lax.axis_size("member")
    entries = rows_dev * lax.axis_size("fsdp") * feature_width
    rows_piece = rows_dev // n_member
    n_part = 2 if rows_piece % 32 == 0 else 1
    rows_part = rows_piece // n_part
    me = lax.axis_index("member")
    me_table = me[None]
    flips = range(1, n_member)
    near = [flip for flip in flips if flip == 1]
    far = [2, 3] if n_member == 4 else list(flips)[1:]

    def rows_of(array, flip, first, rows):
        start = (me ^ flip) * rows_piece + first
        return lax.dynamic_slice(array, (0, start, 0), (members_dev, rows, feature_width))

    grads = [{} for _ in range(n_part)]
    work = {}
    last = None

    def finish(arrived, outs):
        flip, first, piece = arrived
        row_block = (((me ^ flip) * rows_piece + first) // piece.shape[1])[None]
        return adamw(row_block, params, first_moment, second_moment, piece, outs)

    def send(array, flip, first, rows, after):
        source = array if after is None else tied(array, after)
        packed = rows_of(source, flip, first, rows).astype(jnp.bfloat16)
        return swap(packed, "member", flip), packed

    rows_first = 16 if n_part > 1 else 0
    head = []
    if rows_first:
        arrived, last = send(params, far[-1], 0, rows_first, None)
        head.append(arrived)
    skips = [rows_first if flip == far[-1] else 0 for flip in far]
    packed = pack_rows(me_table if last is None else tied(me_table, last), params, far, skips)
    for flip, piece in zip(far, packed):
        work[flip] = swap(piece, "member", flip)
    last = packed
    for flip in far[:1]:
        whole, last = send(gradients, flip, 0, rows_piece, last)
        for part in range(n_part):
            grads[part][flip] = whole
    for flip in near:
        last = (last, head)
        work[flip], last = send(params, flip, 0, rows_piece, last)
        whole, last = send(gradients, flip, 0, rows_piece, last)
        for part in range(n_part):
            grads[part][flip] = whole
    gram = local_gram(me_table, params, [work[flip] for flip in flips], head)
    gram = sum_over(tied(gram, last), "fsdp")
    for flip in near:
        gram = gram + swap(gram, "member", flip)
    last = gram
    for part in range(n_part):
        for flip in far[1:]:
            grads[part][flip], last = send(gradients, flip, part * rows_part, rows_part, last)
    gram = sum_over(gram, "member", 2)
    work = [work[flip] for flip in flips]
    grads = [[piece[flip] for flip in flips] for piece in grads]

    kept, back = [], []
    for part in range(n_part):
        cuts = [(0, rows_part)]
        if part == n_part - 1 and rows_part == 32:
            cuts = LAST_CUTS
        *pieces, pair_distance = mix(
            me_table, gram, params, work, head, gradients, grads[part],
            part * rows_part, rows_part, cuts, kept, entries,
        )
        kept = pieces[:1]
        sent = [(flip, 0, pieces[flip]) for flip in near + far[:-1]]
        sent += [(far[-1], first, piece) for (first, _), piece in zip(cuts, pieces[n_member - 1 :])]
        for order, (flip, first, piece) in enumerate(sent):
            if part == 1 and order > 0:
                piece = tied(piece, back[0][2])
            back.append((flip, part * rows_part + first, swap(piece, "member", flip)))
    outs = finish((0, 0, kept[0]), ())
    for arrived in back:
        outs = finish(arrived, outs)
    new_params, new_first, new_second, update, stein_dir = outs
    return (new_params, new_first, new_second, update, stein_dir, pair_distance)


def solution(mesh):
    return jax.shard_map(
        shards,
        mesh=mesh,
        in_specs=(
            P(("groups", "member"), "fsdp", None),
            P(("groups", "member"), "fsdp", None),
            P(("groups", "member"), "fsdp", None),
            P(("groups", "member"), "fsdp", None),
        ),
        out_specs=(
            P(("groups", "member"), "fsdp", None),
            P(("groups", "member"), "fsdp", None),
            P(("groups", "member"), "fsdp", None),
            P(("groups", "member"), "fsdp", None),
            P(("groups", "member"), "fsdp", None),
            P("groups", None),
        ),
        check_vma=False,
    )
```

```python
import functools
import math

import jax
import jax.numpy as jnp
from jax import lax
from jax.experimental import pallas as pl
from jax.experimental.pallas import tpu as pltpu
from jax.sharding import PartitionSpec as P

STEP_COUNT = 100

decay_first = 0.9
decay_second = 0.95
epsilon = 1e-08
learn_rate = 0.001
weight_decay = 0.05

VMEM_BYTES = 48 << 20
LIGHT = pl.CostEstimate(flops=1024, bytes_accessed=1024, transcendentals=0)
STEP = pl.CostEstimate(flops=1024, bytes_accessed=1 << 20, transcendentals=0)


LAST_CUTS = [(0, 16), (16, 16)]


def swap(x, axis, flip):
    return lax.ppermute(x, axis, [(i, i ^ flip) for i in range(lax.axis_size(axis))])


def tied(x, after):
    return lax.optimization_barrier((x, after))[0]


def sum_over(x, axis, stride=1):
    size = lax.axis_size(axis)
    while stride < size:
        if size // stride >= 4:
            one, two, three = (swap(x, axis, flip * stride) for flip in (1, 2, 3))
            x = (x + one) + (two + three)
            stride *= 4
        else:
            x = x + swap(x, axis, stride)
            stride *= 2
    return x


def owner_matrix(me, n_member, members_dev, block_rows, dtype):
    members = n_member * members_dev
    stacked = lax.broadcasted_iota(jnp.int32, (members * block_rows, members), 0)
    column = lax.broadcasted_iota(jnp.int32, (members * block_rows, members), 1)
    slot = stacked // block_rows
    owner = ((slot // members_dev) ^ me) * members_dev + slot % members_dev
    return jnp.where(owner == column, 1.0, 0.0).astype(dtype)


def same_row(size, block_rows):
    left = lax.broadcasted_iota(jnp.int32, (size, size), 0) % block_rows
    right = lax.broadcasted_iota(jnp.int32, (size, size), 1) % block_rows
    return left == right


def stack_pieces(blocks):
    parts = []
    for block in blocks:
        members_dev, block_rows, width = block.shape
        parts.append(block.astype(jnp.bfloat16).reshape(members_dev * block_rows, width))
    return jnp.concatenate(parts, axis=0)


def pieces_of(refs, head_refs, step):
    blocks = [ref[...] for ref in refs]
    for head_ref in head_refs:
        blocks[-1] = jnp.where(step == 0, head_ref[...], blocks[-1])
    return stack_pieces(blocks)


def pack_kernel(me_ref, *refs):
    del me_ref
    for in_ref, out_ref in zip(refs[: len(refs) // 2], refs[len(refs) // 2 :]):
        skip = in_ref.shape[1] - out_ref.shape[1]
        out_ref[...] = in_ref[:, skip:, :].astype(out_ref.dtype)


def pack_rows(me, params, flips, skips):
    members_dev, rows_dev, width = params.shape
    rows = rows_dev // lax.axis_size("member")
    block_members = max(1, members_dev // 2)
    return pl.pallas_call(
        pack_kernel,
        out_shape=[
            jax.ShapeDtypeStruct((members_dev, rows - skip, width), jnp.bfloat16)
            for skip in skips
        ],
        grid_spec=pltpu.PrefetchScalarGridSpec(
            num_scalar_prefetch=1,
            grid=(members_dev // block_members,),
            in_specs=[
                pl.BlockSpec(
                    (block_members, rows, width),
                    lambda i, me_ref, flip=flip: (i, me_ref[0] ^ flip, 0),
                )
                for flip in flips
            ],
            out_specs=[
                pl.BlockSpec((block_members, rows - skip, width), lambda i, me_ref: (i, 0, 0))
                for skip in skips
            ],
        ),
        compiler_params=pltpu.CompilerParams(vmem_limit_bytes=VMEM_BYTES),
        cost_estimate=LIGHT,
        name="pack",
    )(me, *[params] * len(flips))


def gram_kernel(n_member, me_ref, *refs):
    *piece_refs, gram_ref, acc_ref = refs
    step = pl.program_id(0)
    members_dev, block_rows, _ = piece_refs[0].shape

    @pl.when(step == 0)
    def _():
        acc_ref[...] = jnp.zeros_like(acc_ref)

    stacked = pieces_of(piece_refs[:n_member], piece_refs[n_member:], step)
    acc_ref[...] += lax.dot_general(
        stacked, stacked, (((1,), (1,)), ((), ())), preferred_element_type=jnp.float32
    )

    @pl.when(step == pl.num_programs(0) - 1)
    def _():
        size = acc_ref.shape[0]
        owner = owner_matrix(me_ref[0], n_member, members_dev, block_rows, jnp.float32)
        kept = jnp.where(same_row(size, block_rows), acc_ref[...], 0.0)
        half = jnp.dot(kept, owner, precision=lax.Precision.HIGHEST)
        gram_ref[...] = lax.dot_general(
            owner, half, (((0,), (0,)), ((), ())), precision=lax.Precision.HIGHEST
        )


def local_gram(me, params, work_pieces, head):
    members_dev, rows_piece, width = work_pieces[0].shape
    n_member = len(work_pieces) + 1
    members = n_member * members_dev
    block_rows = min(16, rows_piece)
    steps = rows_piece // block_rows
    block = (members_dev, block_rows, width)
    size = members * block_rows
    return pl.pallas_call(
        functools.partial(gram_kernel, n_member),
        out_shape=jax.ShapeDtypeStruct((members, members), jnp.float32),
        grid_spec=pltpu.PrefetchScalarGridSpec(
            num_scalar_prefetch=1,
            grid=(steps,),
            in_specs=[pl.BlockSpec(block, lambda i, me_ref: (0, me_ref[0] * steps + i, 0))]
            + [pl.BlockSpec(block, lambda i, me_ref: (0, i, 0))] * (n_member - 2)
            + [pl.BlockSpec(block, lambda i, me_ref: (0, jnp.maximum(i - len(head), 0), 0))]
            + [pl.BlockSpec(block, lambda i, me_ref: (0, 0, 0))] * len(head),
            out_specs=pl.BlockSpec((members, members), lambda i, me_ref: (0, 0)),
            scratch_shapes=[pltpu.VMEM((size, size), jnp.float32)],
        ),
        compiler_params=pltpu.CompilerParams(vmem_limit_bytes=VMEM_BYTES),
        cost_estimate=LIGHT,
        name="gram",
    )(me, params, *work_pieces, *head)


def distances(gram):
    members = gram.shape[0]
    row = lax.broadcasted_iota(jnp.int32, gram.shape, 0)
    column = lax.broadcasted_iota(jnp.int32, gram.shape, 1)
    diagonal = jnp.where(row == column, gram, 0.0)
    down = jnp.sum(diagonal, axis=1, keepdims=True)
    across = jnp.sum(diagonal, axis=0, keepdims=True)
    return down + across - 2.0 * gram


def mix_kernel(n_member, n_head, cuts, entries, me_ref, gram_ref, *refs):
    work_refs, refs = refs[:n_member], refs[n_member:]
    head_refs, grad_refs = refs[:n_head], refs[n_head : n_head + n_member]
    n_out = n_member - 1 + len(cuts)
    distance_ref, big_ref, rowsum_ref, repulse_ref = refs[-4:]
    out_refs = refs[-4 - n_out : -4]
    members_dev, block_rows, width = out_refs[0].shape
    members = n_member * members_dev
    size = members * block_rows

    @pl.when(pl.program_id(0) == 0)
    def _():
        sqdist = distances(gram_ref[...])
        distance_ref[...] = sqdist / entries
        total = jnp.sum(jnp.sum(sqdist, axis=1, keepdims=True), axis=0, keepdims=True)
        kernel_scale = total / (members * (members - 1)) / math.log(members)
        kernel_half = jnp.exp(-sqdist / kernel_scale).astype(jnp.bfloat16)
        owner = owner_matrix(me_ref[0], n_member, members_dev, block_rows, jnp.bfloat16)
        tall = jnp.dot(owner, kernel_half, preferred_element_type=jnp.float32)
        square = lax.dot_general(
            tall.astype(jnp.bfloat16), owner, (((1,), (1,)), ((), ())),
            preferred_element_type=jnp.float32,
        )
        big_ref[...] = jnp.where(same_row(size, block_rows), square, 0.0).astype(jnp.bfloat16)
        rowsum_ref[...] = jnp.sum(tall, axis=1, keepdims=True)
        repulse_ref[...] = 2.0 / kernel_scale

    big = big_ref[...]
    work = pieces_of(work_refs, head_refs, pl.program_id(0))
    grads = stack_pieces([ref[...] for ref in grad_refs])
    mixed_grads = jnp.dot(big, grads, preferred_element_type=jnp.float32)
    mixed_work = jnp.dot(big, work, preferred_element_type=jnp.float32)
    stein = (
        repulse_ref[...] * (rowsum_ref[...] * work.astype(jnp.float32) - mixed_work) - mixed_grads
    ) * (1.0 / members)
    stein = stein.reshape(n_member, members_dev, block_rows, width)
    for piece, out_ref in enumerate(out_refs[: n_member - 1]):
        out_ref[...] = stein[piece].astype(jnp.bfloat16)
    for (first, rows), out_ref in zip(cuts, out_refs[n_member - 1 :]):
        if rows >= block_rows and len(cuts) == 1:
            out_ref[...] = stein[-1].astype(jnp.bfloat16)
            continue
        inner = first % block_rows

        @pl.when(pl.program_id(0) == first // block_rows)
        def _():
            out_ref[...] = stein[-1, :, inner : inner + rows].astype(jnp.bfloat16)


def mix(
    me, gram, params, work_pieces, head, gradients, grad_pieces, first_row, rows, cuts, earlier,
    entries,
):
    members_dev, rows_piece, width = work_pieces[0].shape
    n_member = len(work_pieces) + 1
    members = n_member * members_dev
    block_rows = min(16, rows)
    steps = rows // block_rows
    block = (members_dev, block_rows, width)
    size = members * block_rows
    skip = first_row // block_rows
    per_piece = rows_piece // block_rows
    own = pl.BlockSpec(block, lambda i, me_ref: (0, me_ref[0] * per_piece + skip + i, 0))
    whole = pl.BlockSpec(block, lambda i, me_ref: (0, skip + i, 0))
    part = pl.BlockSpec(block, lambda i, me_ref: (0, i, 0))

    def fixed(count):
        return pl.BlockSpec((members_dev, count, width), lambda i, me_ref: (0, 0, 0))

    n_head = len(head)
    late = pl.BlockSpec(block, lambda i, me_ref: (0, jnp.maximum(skip + i - n_head, 0), 0))
    if first_row:
        head = []
    out_rows = [rows if piece else rows_piece for piece in range(n_member - 1)]
    out_rows += [count for _, count in cuts]
    return pl.pallas_call(
        functools.partial(mix_kernel, n_member, len(head), cuts, entries),
        out_shape=[
            jax.ShapeDtypeStruct((members_dev, count, width), jnp.bfloat16) for count in out_rows
        ]
        + [jax.ShapeDtypeStruct((members, members), jnp.float32)],
        grid_spec=pltpu.PrefetchScalarGridSpec(
            num_scalar_prefetch=1,
            grid=(steps,),
            in_specs=[pl.BlockSpec((members, members), lambda i, me_ref: (0, 0)), own]
            + [whole] * (n_member - 2)
            + [late]
            + [fixed(block_rows)] * len(head)
            + [own]
            + [part if piece.shape[1] == rows else whole for piece in grad_pieces]
            + [pl.BlockSpec(memory_space=pl.ANY)] * len(earlier),
            out_specs=[part if piece else whole for piece in range(n_member - 1)]
            + [part if len(cuts) == 1 else fixed(count) for _, count in cuts]
            + [pl.BlockSpec((members, members), lambda i, me_ref: (0, 0))],
            scratch_shapes=[
                pltpu.VMEM((size, size), jnp.bfloat16),
                pltpu.VMEM((size, 1), jnp.float32),
                pltpu.VMEM((1, 1), jnp.float32),
            ],
        ),
        input_output_aliases={
            2 + 2 * n_member + len(head) + idx: idx for idx in range(len(earlier))
        },
        compiler_params=pltpu.CompilerParams(vmem_limit_bytes=VMEM_BYTES),
        cost_estimate=LIGHT,
        name="mix",
    )(me, gram, params, *work_pieces, *head, gradients, *grad_pieces, *earlier)


def adamw_kernel(n_pieces, row_ref, params_ref, first_ref, second_ref, *refs):
    del row_ref
    new_params_ref, new_first_ref, new_second_ref, update_ref, stein_dir_ref = refs[-5:]
    stein = refs[0][...]
    for piece in range(1, n_pieces):
        stein = jnp.where(pl.program_id(0) >= piece, refs[piece][...], stein)
    params = params_ref[...]
    stein_dir = stein.astype(jnp.float32)
    new_first = decay_first * first_ref[...] - (1.0 - decay_first) * stein_dir
    new_second = decay_second * second_ref[...] + (1.0 - decay_second) * stein_dir * stein_dir
    first_hat = new_first * (1.0 / (1.0 - decay_first**STEP_COUNT))
    second_hat = new_second * (1.0 / (1.0 - decay_second**STEP_COUNT))
    update = first_hat / (jnp.sqrt(second_hat) + epsilon) + weight_decay * params
    new_params_ref[...] = params - learn_rate * update
    new_first_ref[...] = new_first
    new_second_ref[...] = new_second
    update_ref[...] = update
    stein_dir_ref[...] = stein_dir


def adamw(row_blocks, params, first_moment, second_moment, pieces, earlier):
    members_dev, rows, width = pieces[0].shape
    block_members = math.gcd(members_dev, 4 if rows > 16 and len(pieces) == 1 else 8)
    block_rows = rows if rows != 16 else 8
    block = (block_members, block_rows, width)
    outer, inner = members_dev // block_members, rows // block_rows

    def home_index(q, i, j, row_ref):
        return (i, row_ref[q] * inner + j, 0)

    def piece_spec(piece):
        def index(q, i, j, row_ref):
            away = jnp.where(q < piece, 0, outer - 1), jnp.where(q < piece, 0, inner - 1)
            return (jnp.where(q == piece, i, away[0]), jnp.where(q == piece, j, away[1]), 0)

        return pl.BlockSpec(block, index)

    home = pl.BlockSpec(block, home_index)
    shape = jax.ShapeDtypeStruct(params.shape, jnp.float32)
    return pl.pallas_call(
        functools.partial(adamw_kernel, len(pieces)),
        out_shape=[shape] * 5,
        grid_spec=pltpu.PrefetchScalarGridSpec(
            num_scalar_prefetch=1,
            grid=(len(pieces), outer, inner),
            in_specs=[home] * 3
            + [piece_spec(piece) for piece in range(len(pieces))]
            + [pl.BlockSpec(memory_space=pl.ANY)] * len(earlier),
            out_specs=[home] * 5,
        ),
        input_output_aliases={4 + len(pieces) + idx: idx for idx in range(len(earlier))},
        compiler_params=pltpu.CompilerParams(vmem_limit_bytes=VMEM_BYTES),
        cost_estimate=STEP,
        name="adamw",
    )(row_blocks, params, first_moment, second_moment, *pieces, *earlier)


def shards(params, gradients, first_moment, second_moment):
    members_dev, rows_dev, feature_width = params.shape
    n_member = lax.axis_size("member")
    entries = rows_dev * lax.axis_size("fsdp") * feature_width
    rows_piece = rows_dev // n_member
    n_part = 2 if rows_piece % 32 == 0 else 1
    rows_part = rows_piece // n_part
    me = lax.axis_index("member")
    me_table = me[None]
    flips = range(1, n_member)
    near = [flip for flip in flips if flip == 1]
    far = [2, 3] if n_member == 4 else list(flips)[1:]

    def rows_of(array, flip, first, rows):
        start = (me ^ flip) * rows_piece + first
        return lax.dynamic_slice(array, (0, start, 0), (members_dev, rows, feature_width))

    grads = [{} for _ in range(n_part)]
    work = {}
    last = None

    def finish(group, outs):
        blocks = [((me ^ flip) * rows_piece + first) // piece.shape[1] for flip, first, piece in group]
        pieces = [piece for _, _, piece in group]
        return adamw(
            jnp.stack(blocks), params, first_moment, second_moment, pieces, outs
        )

    def send(array, flip, first, rows, after):
        source = array if after is None else tied(array, after)
        packed = rows_of(source, flip, first, rows).astype(jnp.bfloat16)
        return swap(packed, "member", flip), packed

    rows_first = 16 if n_part > 1 else 0
    head = []
    if rows_first:
        arrived, last = send(params, far[-1], 0, rows_first, None)
        head.append(arrived)
    skips = [rows_first if flip == far[-1] else 0 for flip in far]
    packed = pack_rows(me_table if last is None else tied(me_table, last), params, far, skips)
    for flip, piece in zip(far, packed):
        work[flip] = swap(piece, "member", flip)
    last = packed
    for flip in far[:1]:
        whole, last = send(gradients, flip, 0, rows_piece, last)
        for part in range(n_part):
            grads[part][flip] = whole
    for flip in near:
        last = (last, head)
        work[flip], last = send(params, flip, 0, rows_piece, last)
        whole, last = send(gradients, flip, 0, rows_piece, last)
        for part in range(n_part):
            grads[part][flip] = whole
    gram = local_gram(me_table, params, [work[flip] for flip in flips], head)
    gram = sum_over(tied(gram, last), "fsdp")
    for flip in near:
        gram = gram + swap(gram, "member", flip)
    last = gram
    for part in range(n_part):
        for flip in far[1:]:
            grads[part][flip], last = send(gradients, flip, part * rows_part, rows_part, last)
    gram = sum_over(gram, "member", 2)
    work = [work[flip] for flip in flips]
    grads = [[piece[flip] for flip in flips] for piece in grads]

    kept, back = [], []
    for part in range(n_part):
        cuts = [(0, rows_part)]
        if part == n_part - 1 and rows_part == 32:
            cuts = LAST_CUTS
        *pieces, pair_distance = mix(
            me_table, gram, params, work, head, gradients, grads[part],
            part * rows_part, rows_part, cuts, kept, entries,
        )
        kept = pieces[:1]
        sent = [(flip, 0, pieces[flip]) for flip in near + far[:-1]]
        sent += [(far[-1], first, piece) for (first, _), piece in zip(cuts, pieces[n_member - 1 :])]
        for order, (flip, first, piece) in enumerate(sent):
            if part == 1 and order > 0:
                piece = tied(piece, back[0][2])
            back.append((flip, part * rows_part + first, swap(piece, "member", flip)))
    groups = [[(0, 0, kept[0])]]
    for idx, arrived in enumerate(back):
        if n_part > 1 and idx in (2, 4) and arrived[2].shape == back[idx - 1][2].shape:
            groups[-1].append(arrived)
        else:
            groups.append([arrived])
    outs = ()
    for group in groups:
        outs = finish(group, outs)
    new_params, new_first, new_second, update, stein_dir = outs
    return (new_params, new_first, new_second, update, stein_dir, pair_distance)


def solution(mesh):
    return jax.shard_map(
        shards,
        mesh=mesh,
        in_specs=(
            P(("groups", "member"), "fsdp", None),
            P(("groups", "member"), "fsdp", None),
            P(("groups", "member"), "fsdp", None),
            P(("groups", "member"), "fsdp", None),
        ),
        out_specs=(
            P(("groups", "member"), "fsdp", None),
            P(("groups", "member"), "fsdp", None),
            P(("groups", "member"), "fsdp", None),
            P(("groups", "member"), "fsdp", None),
            P(("groups", "member"), "fsdp", None),
            P("groups", None),
        ),
        check_vma=False,
    )
```

```python
import functools
import math

import jax
import jax.numpy as jnp
from jax import lax
from jax.experimental import pallas as pl
from jax.experimental.pallas import tpu as pltpu
from jax.sharding import PartitionSpec as P

STEP_COUNT = 100

decay_first = 0.9
decay_second = 0.95
epsilon = 1e-08
learn_rate = 0.001
weight_decay = 0.05

VMEM_BYTES = 48 << 20
LIGHT = pl.CostEstimate(flops=1024, bytes_accessed=1024, transcendentals=0)
STEP = pl.CostEstimate(flops=1024, bytes_accessed=1 << 20, transcendentals=0)


LAST_CUTS = [(0, 16), (16, 16)]


def swap(x, axis, flip):
    return lax.ppermute(x, axis, [(i, i ^ flip) for i in range(lax.axis_size(axis))])


def tied(x, after):
    return lax.optimization_barrier((x, after))[0]


def sum_over(x, axis, stride=1):
    size = lax.axis_size(axis)
    while stride < size:
        if size // stride >= 4:
            one, two, three = (swap(x, axis, flip * stride) for flip in (1, 2, 3))
            x = (x + one) + (two + three)
            stride *= 4
        else:
            x = x + swap(x, axis, stride)
            stride *= 2
    return x


def owner_matrix(me, n_member, members_dev, block_rows, dtype):
    members = n_member * members_dev
    stacked = lax.broadcasted_iota(jnp.int32, (members * block_rows, members), 0)
    column = lax.broadcasted_iota(jnp.int32, (members * block_rows, members), 1)
    slot = stacked // block_rows
    owner = ((slot // members_dev) ^ me) * members_dev + slot % members_dev
    return jnp.where(owner == column, 1.0, 0.0).astype(dtype)


def same_row(size, block_rows):
    left = lax.broadcasted_iota(jnp.int32, (size, size), 0) % block_rows
    right = lax.broadcasted_iota(jnp.int32, (size, size), 1) % block_rows
    return left == right


def stack_pieces(blocks):
    parts = []
    for block in blocks:
        members_dev, block_rows, width = block.shape
        parts.append(block.astype(jnp.bfloat16).reshape(members_dev * block_rows, width))
    return jnp.concatenate(parts, axis=0)


def pieces_of(refs, head_refs, step):
    blocks = [ref[...] for ref in refs]
    for head_ref in head_refs:
        blocks[-1] = jnp.where(step == 0, head_ref[...], blocks[-1])
    return stack_pieces(blocks)


def pack_kernel(me_ref, *refs):
    del me_ref
    for in_ref, out_ref in zip(refs[: len(refs) // 2], refs[len(refs) // 2 :]):
        skip = in_ref.shape[1] - out_ref.shape[1]
        out_ref[...] = in_ref[:, skip:, :].astype(out_ref.dtype)


def pack_rows(me, params, flips, skips):
    members_dev, rows_dev, width = params.shape
    rows = rows_dev // lax.axis_size("member")
    block_members = max(1, members_dev // 2)
    return pl.pallas_call(
        pack_kernel,
        out_shape=[
            jax.ShapeDtypeStruct((members_dev, rows - skip, width), jnp.bfloat16)
            for skip in skips
        ],
        grid_spec=pltpu.PrefetchScalarGridSpec(
            num_scalar_prefetch=1,
            grid=(members_dev // block_members,),
            in_specs=[
                pl.BlockSpec(
                    (block_members, rows, width),
                    lambda i, me_ref, flip=flip: (i, me_ref[0] ^ flip, 0),
                )
                for flip in flips
            ],
            out_specs=[
                pl.BlockSpec((block_members, rows - skip, width), lambda i, me_ref: (i, 0, 0))
                for skip in skips
            ],
        ),
        compiler_params=pltpu.CompilerParams(vmem_limit_bytes=VMEM_BYTES),
        cost_estimate=LIGHT,
        name="pack",
    )(me, *[params] * len(flips))


def gram_kernel(n_member, me_ref, *refs):
    *piece_refs, gram_ref, acc_ref = refs
    step = pl.program_id(0)
    members_dev, block_rows, _ = piece_refs[0].shape

    @pl.when(step == 0)
    def _():
        acc_ref[...] = jnp.zeros_like(acc_ref)

    stacked = pieces_of(piece_refs[:n_member], piece_refs[n_member:], step)
    acc_ref[...] += lax.dot_general(
        stacked, stacked, (((1,), (1,)), ((), ())), preferred_element_type=jnp.float32
    )

    @pl.when(step == pl.num_programs(0) - 1)
    def _():
        size = acc_ref.shape[0]
        owner = owner_matrix(me_ref[0], n_member, members_dev, block_rows, jnp.float32)
        kept = jnp.where(same_row(size, block_rows), acc_ref[...], 0.0)
        half = jnp.dot(kept, owner, precision=lax.Precision.HIGHEST)
        gram_ref[...] = lax.dot_general(
            owner, half, (((0,), (0,)), ((), ())), precision=lax.Precision.HIGHEST
        )


def local_gram(me, params, work_pieces, head):
    members_dev, rows_piece, width = work_pieces[0].shape
    n_member = len(work_pieces) + 1
    members = n_member * members_dev
    block_rows = min(16, rows_piece)
    steps = rows_piece // block_rows
    block = (members_dev, block_rows, width)
    size = members * block_rows
    return pl.pallas_call(
        functools.partial(gram_kernel, n_member),
        out_shape=jax.ShapeDtypeStruct((members, members), jnp.float32),
        grid_spec=pltpu.PrefetchScalarGridSpec(
            num_scalar_prefetch=1,
            grid=(steps,),
            in_specs=[pl.BlockSpec(block, lambda i, me_ref: (0, me_ref[0] * steps + i, 0))]
            + [pl.BlockSpec(block, lambda i, me_ref: (0, i, 0))] * (n_member - 2)
            + [pl.BlockSpec(block, lambda i, me_ref: (0, jnp.maximum(i - len(head), 0), 0))]
            + [pl.BlockSpec(block, lambda i, me_ref: (0, 0, 0))] * len(head),
            out_specs=pl.BlockSpec((members, members), lambda i, me_ref: (0, 0)),
            scratch_shapes=[pltpu.VMEM((size, size), jnp.float32)],
        ),
        compiler_params=pltpu.CompilerParams(vmem_limit_bytes=VMEM_BYTES),
        cost_estimate=LIGHT,
        name="gram",
    )(me, params, *work_pieces, *head)


def distances(gram):
    members = gram.shape[0]
    row = lax.broadcasted_iota(jnp.int32, gram.shape, 0)
    column = lax.broadcasted_iota(jnp.int32, gram.shape, 1)
    diagonal = jnp.where(row == column, gram, 0.0)
    down = jnp.sum(diagonal, axis=1, keepdims=True)
    across = jnp.sum(diagonal, axis=0, keepdims=True)
    return down + across - 2.0 * gram


def mix_kernel(n_member, n_head, cuts, entries, me_ref, gram_ref, *refs):
    work_refs, refs = refs[:n_member], refs[n_member:]
    head_refs, grad_refs = refs[:n_head], refs[n_head : n_head + n_member]
    n_out = n_member - 1 + len(cuts)
    distance_ref, big_ref, rowsum_ref, repulse_ref = refs[-4:]
    out_refs = refs[-4 - n_out : -4]
    members_dev, block_rows, width = out_refs[0].shape
    members = n_member * members_dev
    size = members * block_rows

    @pl.when(pl.program_id(0) == 0)
    def _():
        sqdist = distances(gram_ref[...])
        distance_ref[...] = sqdist / entries
        total = jnp.sum(jnp.sum(sqdist, axis=1, keepdims=True), axis=0, keepdims=True)
        kernel_scale = total / (members * (members - 1)) / math.log(members)
        kernel_half = jnp.exp(-sqdist / kernel_scale).astype(jnp.bfloat16)
        owner = owner_matrix(me_ref[0], n_member, members_dev, block_rows, jnp.bfloat16)
        tall = jnp.dot(owner, kernel_half, preferred_element_type=jnp.float32)
        square = lax.dot_general(
            tall.astype(jnp.bfloat16), owner, (((1,), (1,)), ((), ())),
            preferred_element_type=jnp.float32,
        )
        big_ref[...] = jnp.where(same_row(size, block_rows), square, 0.0).astype(jnp.bfloat16)
        rowsum_ref[...] = jnp.sum(tall, axis=1, keepdims=True)
        repulse_ref[...] = 2.0 / kernel_scale

    big = big_ref[...]
    work = pieces_of(work_refs, head_refs, pl.program_id(0))
    grads = stack_pieces([ref[...] for ref in grad_refs])
    mixed_grads = jnp.dot(big, grads, preferred_element_type=jnp.float32)
    mixed_work = jnp.dot(big, work, preferred_element_type=jnp.float32)
    stein = (
        repulse_ref[...] * (rowsum_ref[...] * work.astype(jnp.float32) - mixed_work) - mixed_grads
    ) * (1.0 / members)
    stein = stein.reshape(n_member, members_dev, block_rows, width)
    for piece, out_ref in enumerate(out_refs[: n_member - 1]):
        out_ref[...] = stein[piece].astype(jnp.bfloat16)
    for (first, rows), out_ref in zip(cuts, out_refs[n_member - 1 :]):
        if rows >= block_rows and len(cuts) == 1:
            out_ref[...] = stein[-1].astype(jnp.bfloat16)
            continue
        inner = first % block_rows

        @pl.when(pl.program_id(0) == first // block_rows)
        def _():
            out_ref[...] = stein[-1, :, inner : inner + rows].astype(jnp.bfloat16)


def mix(
    me, gram, params, work_pieces, head, gradients, grad_pieces, first_row, rows, cuts, earlier,
    entries,
):
    members_dev, rows_piece, width = work_pieces[0].shape
    n_member = len(work_pieces) + 1
    members = n_member * members_dev
    block_rows = min(16, rows)
    steps = rows // block_rows
    block = (members_dev, block_rows, width)
    size = members * block_rows
    skip = first_row // block_rows
    per_piece = rows_piece // block_rows
    own = pl.BlockSpec(block, lambda i, me_ref: (0, me_ref[0] * per_piece + skip + i, 0))
    whole = pl.BlockSpec(block, lambda i, me_ref: (0, skip + i, 0))
    part = pl.BlockSpec(block, lambda i, me_ref: (0, i, 0))

    def fixed(count):
        return pl.BlockSpec((members_dev, count, width), lambda i, me_ref: (0, 0, 0))

    n_head = len(head)
    late = pl.BlockSpec(block, lambda i, me_ref: (0, jnp.maximum(skip + i - n_head, 0), 0))
    if first_row:
        head = []
    out_rows = [rows if piece else rows_piece for piece in range(n_member - 1)]
    out_rows += [count for _, count in cuts]
    return pl.pallas_call(
        functools.partial(mix_kernel, n_member, len(head), cuts, entries),
        out_shape=[
            jax.ShapeDtypeStruct((members_dev, count, width), jnp.bfloat16) for count in out_rows
        ]
        + [jax.ShapeDtypeStruct((members, members), jnp.float32)],
        grid_spec=pltpu.PrefetchScalarGridSpec(
            num_scalar_prefetch=1,
            grid=(steps,),
            in_specs=[pl.BlockSpec((members, members), lambda i, me_ref: (0, 0)), own]
            + [whole] * (n_member - 2)
            + [late]
            + [fixed(block_rows)] * len(head)
            + [own]
            + [part if piece.shape[1] == rows else whole for piece in grad_pieces]
            + [pl.BlockSpec(memory_space=pl.ANY)] * len(earlier),
            out_specs=[part if piece else whole for piece in range(n_member - 1)]
            + [part if len(cuts) == 1 else fixed(count) for _, count in cuts]
            + [pl.BlockSpec((members, members), lambda i, me_ref: (0, 0))],
            scratch_shapes=[
                pltpu.VMEM((size, size), jnp.bfloat16),
                pltpu.VMEM((size, 1), jnp.float32),
                pltpu.VMEM((1, 1), jnp.float32),
            ],
        ),
        input_output_aliases={
            2 + 2 * n_member + len(head) + idx: idx for idx in range(len(earlier))
        },
        compiler_params=pltpu.CompilerParams(vmem_limit_bytes=VMEM_BYTES),
        cost_estimate=LIGHT,
        name="mix",
    )(me, gram, params, *work_pieces, *head, gradients, *grad_pieces, *earlier)


def adamw_kernel(n_pieces, row_ref, params_ref, first_ref, second_ref, *refs):
    del row_ref
    new_params_ref, new_first_ref, new_second_ref, update_ref, stein_dir_ref = refs[-5:]
    stein = refs[0][...]
    for piece in range(1, n_pieces):
        stein = jnp.where(pl.program_id(0) >= piece, refs[piece][...], stein)
    params = params_ref[...]
    stein_dir = stein.astype(jnp.float32)
    new_first = decay_first * first_ref[...] - (1.0 - decay_first) * stein_dir
    new_second = decay_second * second_ref[...] + (1.0 - decay_second) * stein_dir * stein_dir
    first_hat = new_first * (1.0 / (1.0 - decay_first**STEP_COUNT))
    second_hat = new_second * (1.0 / (1.0 - decay_second**STEP_COUNT))
    update = first_hat / (jnp.sqrt(second_hat) + epsilon) + weight_decay * params
    new_params_ref[...] = params - learn_rate * update
    new_first_ref[...] = new_first
    new_second_ref[...] = new_second
    update_ref[...] = update
    stein_dir_ref[...] = stein_dir


def adamw(row_blocks, params, first_moment, second_moment, pieces, earlier):
    members_dev, rows, width = pieces[0].shape
    block_members = math.gcd(members_dev, 4 if rows > 16 and len(pieces) == 1 else 8)
    block_rows = rows if rows != 16 else 8
    block = (block_members, block_rows, width)
    outer, inner = members_dev // block_members, rows // block_rows

    def home_index(q, i, j, row_ref):
        return (i, row_ref[q] * inner + j, 0)

    def piece_spec(piece):
        def index(q, i, j, row_ref):
            away = jnp.where(q < piece, 0, outer - 1), jnp.where(q < piece, 0, inner - 1)
            return (jnp.where(q == piece, i, away[0]), jnp.where(q == piece, j, away[1]), 0)

        return pl.BlockSpec(block, index)

    home = pl.BlockSpec(block, home_index)
    shape = jax.ShapeDtypeStruct(params.shape, jnp.float32)
    return pl.pallas_call(
        functools.partial(adamw_kernel, len(pieces)),
        out_shape=[shape] * 5,
        grid_spec=pltpu.PrefetchScalarGridSpec(
            num_scalar_prefetch=1,
            grid=(len(pieces), outer, inner),
            in_specs=[home] * 3
            + [piece_spec(piece) for piece in range(len(pieces))]
            + [pl.BlockSpec(memory_space=pl.ANY)] * len(earlier),
            out_specs=[home] * 5,
        ),
        input_output_aliases={4 + len(pieces) + idx: idx for idx in range(len(earlier))},
        compiler_params=pltpu.CompilerParams(vmem_limit_bytes=VMEM_BYTES),
        cost_estimate=STEP,
        name="adamw",
    )(row_blocks, params, first_moment, second_moment, *pieces, *earlier)


def shards(params, gradients, first_moment, second_moment):
    members_dev, rows_dev, feature_width = params.shape
    n_member = lax.axis_size("member")
    entries = rows_dev * lax.axis_size("fsdp") * feature_width
    rows_piece = rows_dev // n_member
    n_part = 2 if rows_piece % 32 == 0 else 1
    rows_part = rows_piece // n_part
    me = lax.axis_index("member")
    me_table = me[None]
    flips = range(1, n_member)
    near = [flip for flip in flips if flip == 1]
    far = [2, 3] if n_member == 4 else list(flips)[1:]

    def rows_of(array, flip, first, rows):
        start = (me ^ flip) * rows_piece + first
        return lax.dynamic_slice(array, (0, start, 0), (members_dev, rows, feature_width))

    grads = [{} for _ in range(n_part)]
    work = {}
    last = None

    def finish(group, outs):
        blocks = [((me ^ flip) * rows_piece + first) // piece.shape[1] for flip, first, piece in group]
        pieces = [piece for _, _, piece in group]
        return adamw(
            jnp.stack(blocks), params, first_moment, second_moment, pieces, outs
        )

    def send(array, flip, first, rows, after):
        source = array if after is None else tied(array, after)
        packed = rows_of(source, flip, first, rows).astype(jnp.bfloat16)
        return swap(packed, "member", flip), packed

    rows_first = 16 if n_part > 1 else 0
    head = []
    if rows_first:
        arrived, last = send(params, far[-1], 0, rows_first, None)
        head.append(arrived)
    skips = [rows_first if flip == far[-1] else 0 for flip in far]
    packed = pack_rows(me_table if last is None else tied(me_table, last), params, far, skips)
    for flip, piece in zip(far, packed):
        work[flip] = swap(piece, "member", flip)
    last = packed
    for flip in far[:1]:
        whole, last = send(gradients, flip, 0, rows_piece, last)
        for part in range(n_part):
            grads[part][flip] = whole
    for flip in near:
        last = (last, head)
        work[flip], last = send(params, flip, 0, rows_piece, last)
        whole, last = send(gradients, flip, 0, rows_piece, last)
        for part in range(n_part):
            grads[part][flip] = whole
    gram = local_gram(me_table, params, [work[flip] for flip in flips], head)
    gram = sum_over(tied(gram, last), "fsdp")
    for flip in near:
        gram = gram + swap(gram, "member", flip)
    last = gram
    for part in range(n_part):
        for flip in far[1:]:
            grads[part][flip], last = send(gradients, flip, part * rows_part, rows_part, last)
    gram = sum_over(gram, "member", 2)
    work = [work[flip] for flip in flips]
    grads = [[piece[flip] for flip in flips] for piece in grads]

    kept, back = [], []
    for part in range(n_part):
        cuts = [(0, rows_part)]
        if part == n_part - 1 and rows_part == 32:
            cuts = LAST_CUTS
        *pieces, pair_distance = mix(
            me_table, gram, params, work, head, gradients, grads[part],
            part * rows_part, rows_part, cuts, kept, entries,
        )
        kept = pieces[:1]
        sent = [(flip, 0, pieces[flip]) for flip in near + far[:-1]]
        sent += [(far[-1], first, piece) for (first, _), piece in zip(cuts, pieces[n_member - 1 :])]
        for order, (flip, first, piece) in enumerate(sent):
            if part == 1 and order > 0:
                piece = tied(piece, back[0][2])
            back.append((flip, part * rows_part + first, swap(piece, "member", flip)))
    groups = [[(0, 0, kept[0])]]
    for idx, arrived in enumerate(back):
        if n_part > 1 and idx in (1, 3) and arrived[2].shape == back[idx - 1][2].shape:
            groups[-1].append(arrived)
        else:
            groups.append([arrived])
    outs = ()
    for group in groups:
        outs = finish(group, outs)
    new_params, new_first, new_second, update, stein_dir = outs
    return (new_params, new_first, new_second, update, stein_dir, pair_distance)


def solution(mesh):
    return jax.shard_map(
        shards,
        mesh=mesh,
        in_specs=(
            P(("groups", "member"), "fsdp", None),
            P(("groups", "member"), "fsdp", None),
            P(("groups", "member"), "fsdp", None),
            P(("groups", "member"), "fsdp", None),
        ),
        out_specs=(
            P(("groups", "member"), "fsdp", None),
            P(("groups", "member"), "fsdp", None),
            P(("groups", "member"), "fsdp", None),
            P(("groups", "member"), "fsdp", None),
            P(("groups", "member"), "fsdp", None),
            P("groups", None),
        ),
        check_vma=False,
    )
```
